32 devices in a mesh: replica: 16 (over z, x, core), shard: 2 (over y).
Axes of the slice: x: 2, y: 2, z: 4, core: 2. Of those that a mesh axis runs over, the one named last changes fastest.
Arguments:
- tokens: bfloat16 [8192, 768], P(('replica', 'shard')), may hold values from -32 to 32
- lengths: int32 [32], P(('replica', 'shard')), may hold values from 1 to 256, 5120 in all
- cotangent: bfloat16 [8192, 768], P(('replica', 'shard')), may hold values from -6 to 6
- w_qkv: bfloat16 [768, 2304], P('shard'), may hold values from -0.14433757 to 0.14433757
- bias_q: bfloat16 [768], P('shard'), may hold values from -3 to 3
- bias_v: bfloat16 [768], P('shard'), may hold values from -3 to 3
- w_out: bfloat16 [768, 768], P('shard'), may hold values from -1.75 to 1.75
- bias_out: bfloat16 [768], P('shard'), may hold values from -3 to 3
- gain_attn: bfloat16 [768], P('shard'), may hold values from 0.5 to 1.5
- shift_attn: bfloat16 [768], P('shard'), may hold values from -3 to 3
- w_in: bfloat16 [768, 3072], P('shard'), may hold values from -0.21875 to 0.21875
- bias_in: bfloat16 [3072], P('shard'), may hold values from -3 to 3
- w_back: bfloat16 [3072, 768], P('shard'), may hold values from -0.109375 to 0.109375
- bias_back: bfloat16 [768], P('shard'), may hold values from -3 to 3
- gain_ffn: bfloat16 [768], P('shard'), may hold values from 0.5 to 1.5
- shift_ffn: bfloat16 [768], P('shard'), may hold values from -3 to 3
Outputs:
- block_out: bfloat16 [8192, 768], P(('replica', 'shard'))
- grad_tokens: float32 [8192, 768], P(('replica', 'shard'))
- grad_w_qkv: float32 [768, 2304], P('shard')
- grad_bias_q: float32 [768], P('shard')
- grad_bias_v: float32 [768], P('shard')
- grad_w_out: float32 [768, 768], P('shard')
- grad_bias_out: float32 [768], P('shard')
- grad_gain_attn: float32 [768], P('shard')
- grad_shift_attn: float32 [768], P('shard')
- grad_w_in: float32 [768, 3072], P('shard')
- grad_bias_in: float32 [3072], P('shard')
- grad_w_back: float32 [3072, 768], P('shard')
- grad_bias_back: float32 [768], P('shard')
- grad_gain_ffn: float32 [768], P('shard')
- grad_shift_ffn: float32 [768], P('shard')
The draws below stay inside these ranges and needn't reach their ends.
Inputs may be any that keep to these rules, and one draw needn't show every extreme that they name: `lengths`: each sequence has at least one live token; the longest has exactly 256.
All inputs are finite; a program needn't handle non-finite values. No bound on the sum of `lengths` on one device may be relied on, other than what follows from the above.
Results may differ from the reference program's by a relative error of at most 0.012.
The reference program's roundings to bfloat16 on the way (of `attend`, `context`, `act`, `grad_ctx`, `grad_scores` and `grad_qkv_b`) count: a program that leaves them out, or rounds other values in their place, can miss the bound.
Values may be sent and summed in bfloat16 or wider, within the bound.
A program may use at most 192 MiB of HBM per device.

```python
import math
import jax
import jax.numpy as jnp
import numpy as np
from jax import lax

D = 768
HEADS = 12
HEAD_DIM = 64
FF = 3072
LEN = 256
SEQS = 32
TOKENS = 8192


def draw_tokens(key, part):
    base_key = jax.random.fold_in(key, 0)
    lead_key = jax.random.fold_in(key, 1)
    strength_key = jax.random.fold_in(key, 3)
    base_rows = jnp.clip(jax.random.normal(base_key, (SEQS, LEN, D), jnp.float32), -4.0, 4.0)
    lead_rows = jnp.clip(jax.random.normal(lead_key, (SEQS, 1, D), jnp.float32), -4.0, 4.0)
    strength = jnp.exp(jax.random.uniform(strength_key, (SEQS, 1, 1), jnp.float32, math.log(3.0), math.log(8.0)))
    position = jnp.arange(LEN, dtype=jnp.int32)[None, :, None]
    feature = jnp.arange(D, dtype=jnp.int32)[None, None, :]
    paired = (position < 2) & (feature < D // 2)
    drawn = jnp.where(paired, lead_rows * strength, base_rows)
    return drawn.reshape(TOKENS, D).astype(jnp.bfloat16)


def draw_w_qkv(key, part):
    weight_key, head_key = jax.random.split(key)
    entries = jnp.clip(jax.random.normal(weight_key, (D, 3 * D), jnp.float32), -3.9, 3.9)
    entries = entries * D ** (-0.5)
    chosen = jax.random.randint(head_key, (), 0, HEADS)
    row_index = jnp.arange(D, dtype=jnp.int32)[:, None]
    column_index = jnp.arange(D, dtype=jnp.int32)[None, :]
    shared = (column_index // HEAD_DIM == chosen) & (row_index < D // 2)
    query_part = entries[:, :D]
    key_part = jnp.where(shared, query_part, entries[:, D:2 * D])
    return jnp.concatenate([query_part, key_part, entries[:, 2 * D:]], axis=1).astype(jnp.bfloat16)


def level_of(key, shape, cuts, least, largest):
    level = 1.0
    for dim, parts in cuts:
        steps = jax.random.uniform(jax.random.fold_in(jax.random.fold_in(key, 6), dim), (parts,), jnp.float32, least / len(cuts), largest / len(cuts))
        level = level * jnp.repeat(jnp.exp(steps), shape[dim] // parts).reshape((-1,) + (1,) * (len(shape) - 1 - dim))
    return level


def profile(count, total, bound, slope):
    loads = [(1 << 20) // math.isqrt(grade ** slope) + 1 for grade in range(2, count + 1)]
    surplus, holding = total - bound - (count - 1), [1] * (count - 1)
    while surplus > 0:
        movable = [i for i in range(count - 1) if holding[i] < bound]
        mass, budget = sum([loads[i] for i in movable]), surplus
        for i in movable:
            addition = min(bound - holding[i], max(1, budget * loads[i] // mass), surplus)
            holding[i] = holding[i] + addition
            surplus = surplus - addition
    return np.array([bound] + holding)


def uneven(rng, number_of, total, reach, slope):
    if number_of == 2:
        one = jax.random.randint(rng, (), max(1, total - reach), min(reach, total - 1) + 1)
        return jnp.stack([one, total - one])
    tallies = jnp.asarray(profile(number_of, total, reach, slope), jnp.int32)
    pairs = (number_of - 1) // 2
    giver, taker = tallies[1:1 + 2 * pairs:2], tallies[2:2 + 2 * pairs:2]
    slack = jnp.minimum(giver - 1, reach - taker)
    shifted = jax.random.randint(jax.random.fold_in(rng, 1), (pairs,), 0, 1 << 20) % (slack + 1)
    tallies = tallies.at[1:1 + 2 * pairs:2].set(giver - shifted).at[2:2 + 2 * pairs:2].set(taker + shifted)
    return tallies[jax.random.permutation(jax.random.fold_in(rng, 2), number_of)]


def bell_draw(stream_key, extent, spread, limit, shards=(), kind=jnp.bfloat16):
    values = jax.random.normal(stream_key, extent, jnp.float32) * spread
    if len(shards) > 0:
        values = level_of(stream_key, extent, shards, -0.22, 0.18) * values
    return jnp.clip(values, min=-limit, max=limit).astype(kind)


def setup_inputs(seed: int = 0) -> dict:
    streams_of = jax.random.split(jax.random.key(seed), 17)
    return {
        "tokens": draw_tokens(jax.random.fold_in(streams_of[16], 71), 0),
        "lengths": uneven(streams_of[1], SEQS, SEQS * LEN * 5 // 8, LEN, 2).astype(jnp.int32),
        "cotangent": bell_draw(streams_of[2], (TOKENS, D), 1.0, 6.0, ((0, 32),)),
        "w_qkv": draw_w_qkv(jax.random.fold_in(streams_of[16], 71), 0),
        "bias_q": bell_draw(streams_of[4], (D,), 0.5, 3.0, ((0, 2),)),
        "bias_v": bell_draw(streams_of[5], (D,), 0.5, 3.0, ((0, 2),)),
        "w_out": bell_draw(streams_of[6], (D, D), (D // 64) ** -0.5, 1.75, ((0, 2),)),
        "bias_out": bell_draw(streams_of[7], (D,), 0.5, 3.0, ((0, 2),)),
        "gain_attn": jnp.clip(1.0 + 0.1 * jax.random.normal(streams_of[8], (D,), jnp.float32), 0.5, 1.5).astype(jnp.bfloat16),
        "shift_attn": bell_draw(streams_of[9], (D,), 0.5, 3.0, ((0, 2),)),
        "w_in": bell_draw(streams_of[10], (D, FF), D ** -0.5, 0.21875, ((0, 2),)),
        "bias_in": bell_draw(streams_of[11], (FF,), 0.5, 3.0, ((0, 2),)),
        "w_back": bell_draw(streams_of[12], (FF, D), FF ** -0.5, 0.109375, ((0, 2),)),
        "bias_back": bell_draw(streams_of[13], (D,), 0.5, 3.0, ((0, 2),)),
        "gain_ffn": jnp.clip(1.0 + 0.1 * jax.random.normal(streams_of[14], (D,), jnp.float32), 0.5, 1.5).astype(jnp.bfloat16),
        "shift_ffn": bell_draw(streams_of[15], (D,), 0.5, 3.0, ((0, 2),)),
    }


def rounded(value):
    return lax.optimization_barrier(value.astype(jnp.bfloat16)).astype(jnp.float32)

def normalize(hidden):
    average = lax.optimization_barrier(jnp.mean(hidden, axis=-1, keepdims=True))
    centred = hidden - average
    inv_std = lax.rsqrt(lax.optimization_barrier(jnp.mean(centred * centred, axis=-1, keepdims=True)) + 1e-12)
    return (centred * inv_std, inv_std)

def norm_back(grad_in, normed, inv_std, gain):
    grad_norm = grad_in * gain
    return inv_std * (grad_norm - lax.optimization_barrier(jnp.mean(grad_norm, axis=-1, keepdims=True)) - normed * lax.optimization_barrier(jnp.mean(grad_norm * normed, axis=-1, keepdims=True)))

def gelu_slope(pre):
    return 0.5 * (1.0 + lax.erf(pre * 0.7071067811865476)) + pre * jnp.exp(-0.5 * pre * pre) * 0.3989422804014327

def encoder_block(inputs, lens, cotan, params):
    w_qkv, bias_q, bias_v, w_out, bias_out, gain_attn, shift_attn, w_in, bias_in, w_back, bias_back, gain_ffn, shift_ffn = params
    group, span, width = inputs.shape
    scale = HEAD_DIM ** (-0.5)
    live = jnp.arange(span, dtype=jnp.int32)[None, :] < lens[:, None]
    input_f = inputs.astype(jnp.float32)
    qkv = jnp.einsum('bld,de->ble', input_f, w_qkv)
    query = rounded(qkv[..., :D] + bias_q).reshape(group, span, HEADS, HEAD_DIM)
    keys = rounded(qkv[..., D:2 * D]).reshape(group, span, HEADS, HEAD_DIM)
    values = rounded(qkv[..., 2 * D:] + bias_v).reshape(group, span, HEADS, HEAD_DIM)

    def make_scores():
        raw = jnp.einsum('bqhe,bkhe->bhqk', query, keys) * scale
        return jnp.where(live[:, None, None, :], raw, -1000000000.0)
    scores = make_scores()
    top = lax.optimization_barrier(jnp.max(scores, axis=-1, keepdims=True))
    expo = jnp.exp(scores - top)
    total = lax.optimization_barrier(jnp.sum(expo, axis=-1, keepdims=True))
    log_total = top + jnp.log(total)
    attend = rounded(expo / total)
    context = rounded(jnp.einsum('bhqk,bkhe->bqhe', attend, values).reshape(group, span, D))
    resid_one = input_f + jnp.einsum('bld,de->ble', context, w_out) + bias_out
    normed_one, inv_one = normalize(resid_one)
    mid = normed_one * gain_attn + shift_attn
    mid_b = rounded(mid)
    pre = jnp.einsum('bld,df->blf', mid_b, w_in) + bias_in
    act = rounded(0.5 * pre * (1.0 + lax.erf(pre * 0.7071067811865476)))
    resid_two = mid + jnp.einsum('blf,fd->bld', act, w_back) + bias_back
    normed_two, inv_two = normalize(resid_two)
    block_out = (normed_two * gain_ffn + shift_ffn).astype(jnp.bfloat16)
    grad_out = cotan.astype(jnp.float32) * live[..., None].astype(jnp.float32)
    g_gain_ffn = lax.optimization_barrier(jnp.sum(grad_out * normed_two, axis=(0, 1)))
    g_shift_ffn = lax.optimization_barrier(jnp.sum(grad_out, axis=(0, 1)))
    grad_two = norm_back(grad_out, normed_two, inv_two, gain_ffn)
    grad_two_b = rounded(grad_two)
    g_w_back = jnp.einsum('blf,bld->fd', act, grad_two_b)
    g_bias_back = lax.optimization_barrier(jnp.sum(grad_two, axis=(0, 1)))
    grad_pre = jnp.einsum('bld,fd->blf', grad_two_b, w_back) * gelu_slope(pre)
    grad_pre_b = rounded(grad_pre)
    g_w_in = jnp.einsum('bld,blf->df', mid_b, grad_pre_b)
    g_bias_in = lax.optimization_barrier(jnp.sum(grad_pre, axis=(0, 1)))
    grad_mid = grad_two + jnp.einsum('blf,df->bld', grad_pre_b, w_in)
    g_gain_attn = lax.optimization_barrier(jnp.sum(grad_mid * normed_one, axis=(0, 1)))
    g_shift_attn = lax.optimization_barrier(jnp.sum(grad_mid, axis=(0, 1)))
    grad_one = norm_back(grad_mid, normed_one, inv_one, gain_attn)
    grad_one_b = rounded(grad_one)
    g_w_out = jnp.einsum('bld,ble->de', context, grad_one_b)
    g_bias_out = lax.optimization_barrier(jnp.sum(grad_one, axis=(0, 1)))
    grad_ctx = rounded(jnp.einsum('ble,de->bld', grad_one_b, w_out)).reshape(group, span, HEADS, HEAD_DIM)
    weights_again = jnp.exp(make_scores() - log_total)
    weights_b = rounded(weights_again)
    grad_att = jnp.einsum('bqhe,bkhe->bhqk', grad_ctx, values)
    grad_values = jnp.einsum('bhqk,bqhe->bkhe', weights_b, grad_ctx)
    delta = lax.optimization_barrier(jnp.sum(weights_again * grad_att, axis=-1, keepdims=True))
    grad_scores = rounded(weights_again * (grad_att - delta) * scale)
    grad_query = jnp.einsum('bhqk,bkhe->bqhe', grad_scores, keys).reshape(group, span, D)
    grad_keys = jnp.einsum('bhqk,bqhe->bkhe', grad_scores, query).reshape(group, span, D)
    grad_values = grad_values.reshape(group, span, D)
    grad_qkv_b = rounded(jnp.concatenate([grad_query, grad_keys, grad_values], axis=-1))
    g_w_qkv = jnp.einsum('bld,ble->de', input_f, grad_qkv_b)
    g_bias_q = lax.optimization_barrier(jnp.sum(grad_query, axis=(0, 1)))
    g_bias_v = lax.optimization_barrier(jnp.sum(grad_values, axis=(0, 1)))
    grad_input = grad_one + jnp.einsum('ble,de->bld', grad_qkv_b, w_qkv)
    grads = (g_w_qkv, g_bias_q, g_bias_v, g_w_out, g_bias_out, g_gain_attn, g_shift_attn, g_w_in, g_bias_in, g_w_back, g_bias_back, g_gain_ffn, g_shift_ffn)
    return (block_out, grad_input, grads)

def reference(tokens, lengths, cotangent, w_qkv, bias_q, bias_v, w_out, bias_out, gain_attn, shift_attn, w_in, bias_in, w_back, bias_back, gain_ffn, shift_ffn):
    params = tuple((p.astype(jnp.float32) for p in (w_qkv, bias_q, bias_v, w_out, bias_out, gain_attn, shift_attn, w_in, bias_in, w_back, bias_back, gain_ffn, shift_ffn)))
    group = math.gcd(SEQS, max(1, 4096 // LEN))
    count = SEQS // group
    tok_blocks = tokens.reshape(count, group, LEN, D)
    len_blocks = lengths.reshape(count, group).astype(jnp.int32)
    cot_blocks = cotangent.reshape(count, group, LEN, D)
    zeros = tuple((jnp.zeros(p.shape, jnp.float32) for p in params))

    def advance(carry, item):
        out_block, grad_block, grads = encoder_block(item[0], item[1], item[2], params)
        return (tuple((c + g for c, g in zip(carry, grads))), (out_block, grad_block))
    totals, (outs, grad_inputs) = lax.scan(advance, zeros, (tok_blocks, len_blocks, cot_blocks))
    factor = TOKENS ** (-0.5)
    t_qkv, t_bq, t_bv, t_out, t_bo, t_ga, t_sa, t_in, t_bi, t_back, t_bb, t_gf, t_sf = totals
    return (outs.reshape(TOKENS, D), grad_inputs.reshape(TOKENS, D), t_qkv * factor, t_bq * factor, t_bv * factor, t_out * factor, t_bo * factor, t_ga * factor, t_sa * factor, t_in * factor, t_bi * factor, t_back * factor, t_bb * factor, t_gf * factor, t_sf * factor)
```

```python
import jax
import jax.numpy as jnp
from jax import lax
from jax.sharding import PartitionSpec as P

HEADS = 12
HEAD_DIM = 64
ORDERS = (
    ("core", "shard", "x", "z0", "z1", "z2"),
    ("core", "x", "shard", "z0", "z1", "z2"),
    ("core", "shard", "x", "z0", "z1", "z2"),
    ("core", "z0", "shard", "x", "z1", "z2"),
)


def product(form, left, right):
    return jnp.einsum(form, left, right, preferred_element_type=jnp.float32)


def normalize(hidden):
    average = jnp.mean(hidden, axis=-1, keepdims=True)
    centred = hidden - average
    inv_std = lax.rsqrt(jnp.mean(centred * centred, axis=-1, keepdims=True) + 1e-12)
    return (centred * inv_std, inv_std)


def norm_back(grad_in, normed, inv_std, gain):
    grad_norm = grad_in * gain
    return inv_std * (
        grad_norm
        - jnp.mean(grad_norm, axis=-1, keepdims=True)
        - normed * jnp.mean(grad_norm * normed, axis=-1, keepdims=True)
    )


def gelu_slope(pre):
    return (
        0.5 * (1.0 + lax.erf(pre * 0.7071067811865476))
        + pre * jnp.exp(-0.5 * pre * pre) * 0.3989422804014327
    )


def swap(value, axis, size, bit=1):
    return lax.ppermute(value, axis, [(i, i ^ bit) for i in range(size)])


def pick(value, index, dim):
    return lax.dynamic_index_in_dim(value, index, dim, keepdims=True)


def paired(mine, other, bit, dim):
    return jnp.where(
        bit == 0,
        jnp.concatenate([mine, other], axis=dim),
        jnp.concatenate([other, mine], axis=dim),
    )


def gather_weight(block):
    shards = lax.axis_size("shard")
    if shards != 2:
        return lax.all_gather(block, "shard", axis=0, tiled=True)
    rows = block.shape[0]
    here, x, core = lax.axis_index("shard"), lax.axis_index("x"), lax.axis_index("core")
    parts = block.reshape(2, 2, rows // 4, block.shape[1])
    mine = pick(pick(parts, x, 0), core, 1)
    far = swap(mine, "shard", 2)
    far = paired(far, swap(far, "x", 2), x, 0)
    far = paired(far, swap(far, "core", 2), core, 1)
    return paired(block, far.reshape(block.shape), here, 0)


def gather_vectors(vectors):
    packed = jnp.concatenate(vectors)
    shards = lax.axis_size("shard")
    if shards == 2:
        both = paired(packed[None], swap(packed, "shard", 2)[None], lax.axis_index("shard"), 0)
    else:
        both = lax.all_gather(packed, "shard", axis=0)
    out, at = [], 0
    for vector in vectors:
        out.append(both[:, at : at + vector.shape[0]].reshape(-1))
        at += vector.shape[0]
    return out


def z_bits():
    return (lax.axis_size("z") - 1).bit_length()


def stage(name):
    if name[0] == "z":
        bit = int(name[1:])
        return "z", lax.axis_size("z"), 1 << bit, (lax.axis_index("z") >> bit) & 1, 3 + bit
    return name, 2, 1, lax.axis_index(name), {"shard": 0, "core": 1, "x": 2}[name]


def reduce_weight(grad, order):
    bf16, f32 = jnp.bfloat16, jnp.float32
    shards, bits = lax.axis_size("shard"), z_bits()
    parts = 4 * lax.axis_size("z")
    rows, columns = grad.shape[0] // shards, grad.shape[1]
    held = grad.reshape((shards, 2, 2) + (2,) * bits + (rows // parts, columns))
    order = [name for name in order if name[0] != "z" or int(name[1:]) < bits]
    for name in order:
        if name == "shard" and shards != 2:
            held = lax.psum_scatter(held.astype(f32), "shard", scatter_dimension=0, tiled=True)
            continue
        axis, size, hop, bit, dim = stage(name)
        arrived = swap(pick(held, 1 - bit, dim).astype(bf16), axis, size, hop)
        held = pick(held, bit, dim).astype(f32) + arrived.astype(f32)
    held = held.astype(bf16)
    for name in reversed(order):
        if name != "shard":
            axis, size, hop, bit, dim = stage(name)
            held = paired(held, swap(held, axis, size, hop), bit, dim)
    return held.reshape(rows, columns).astype(f32)


def reduce_vectors(vectors):
    shards = lax.axis_size("shard")
    packed = jnp.concatenate([v.reshape(shards, -1) for v in vectors], axis=1)
    for name in ["core", "x"] + [f"z{b}" for b in range(z_bits())]:
        axis, size, hop, _, _ = stage(name)
        packed = packed + swap(packed, axis, size, hop)
    if shards == 2:
        here = lax.axis_index("shard")
        total = pick(packed, here, 0) + swap(pick(packed, 1 - here, 0), "shard", 2)
    else:
        total = lax.psum_scatter(packed, "shard", scatter_dimension=0, tiled=True)
    total = total.reshape(-1)
    out, at = [], 0
    for vector in vectors:
        size = vector.shape[0] // shards
        out.append(total[at : at + size])
        at += size
    return out


def on_device(
    tokens,
    lengths,
    cotangent,
    w_qkv,
    bias_q,
    bias_v,
    w_out,
    bias_out,
    gain_attn,
    shift_attn,
    w_in,
    bias_in,
    w_back,
    bias_back,
    gain_ffn,
    shift_ffn,
):
    bf16 = jnp.bfloat16
    f32 = jnp.float32
    f_bq, f_bv, f_bo, f_ga, f_sa, f_bi, f_bb, f_gf, f_sf = gather_vectors(
        (bias_q, bias_v, bias_out, gain_attn, shift_attn, bias_in, bias_back, gain_ffn, shift_ffn)
    )
    f_qkv = gather_weight(w_qkv)
    f_out = gather_weight(w_out)
    f_in = gather_weight(w_in)
    f_back = gather_weight(w_back)
    group = lengths.shape[0]
    span = tokens.shape[0] // group
    width = tokens.shape[1]
    scale = HEAD_DIM ** (-0.5)
    factor = float(tokens.shape[0] * lax.axis_size(("z", "x", "core", "shard"))) ** (-0.5)
    live = jnp.arange(span, dtype=jnp.int32)[None, :] < lengths[:, None]
    inputs = tokens.reshape(group, span, width)
    qkv = product("bld,de->ble", inputs, f_qkv)
    query = (qkv[..., :width] + f_bq.astype(f32)).astype(bf16).reshape(group, span, HEADS, HEAD_DIM)
    keys = qkv[..., width : 2 * width].astype(bf16).reshape(group, span, HEADS, HEAD_DIM)
    values = (
        (qkv[..., 2 * width :] + f_bv.astype(f32))
        .astype(bf16)
        .reshape(group, span, HEADS, HEAD_DIM)
    )

    def make_scores():
        raw = product("bqhe,bkhe->bhqk", query, keys) * scale
        return jnp.where(live[:, None, None, :], raw, -1000000000.0)

    scores = make_scores()
    top = jnp.max(scores, axis=-1, keepdims=True)
    expo = jnp.exp(scores - top)
    total = jnp.sum(expo, axis=-1, keepdims=True)
    log_total = top + jnp.log(total)
    attend = (expo / total).astype(bf16)
    context = product("bhqk,bkhe->bqhe", attend, values).reshape(group, span, width).astype(bf16)
    resid_one = inputs.astype(f32) + product("bld,de->ble", context, f_out) + f_bo.astype(f32)
    normed_one, inv_one = normalize(resid_one)
    gain_one = f_ga.astype(f32)
    mid = normed_one * gain_one + f_sa.astype(f32)
    mid_b = mid.astype(bf16)
    pre = product("bld,df->blf", mid_b, f_in) + f_bi.astype(f32)
    act = (0.5 * pre * (1.0 + lax.erf(pre * 0.7071067811865476))).astype(bf16)
    resid_two = mid + product("blf,fd->bld", act, f_back) + f_bb.astype(f32)
    normed_two, inv_two = normalize(resid_two)
    gain_two = f_gf.astype(f32)
    block_out = (normed_two * gain_two + f_sf.astype(f32)).astype(bf16)
    b_qkv, b_out, b_in, b_back = f_qkv, f_out, f_in, f_back
    grad_out = cotangent.reshape(group, span, width).astype(f32) * live[..., None].astype(f32)
    g_gain_ffn = jnp.sum(grad_out * normed_two, axis=(0, 1))
    g_shift_ffn = jnp.sum(grad_out, axis=(0, 1))
    grad_two = norm_back(grad_out, normed_two, inv_two, gain_two)
    grad_two_b = grad_two.astype(bf16)
    g_w_back = product("blf,bld->fd", act, grad_two_b)
    g_bias_back = jnp.sum(grad_two, axis=(0, 1))
    grad_pre = product("bld,fd->blf", grad_two_b, b_back) * gelu_slope(pre)
    grad_pre_b = grad_pre.astype(bf16)
    g_w_in = product("bld,blf->df", mid_b, grad_pre_b)
    g_bias_in = jnp.sum(grad_pre, axis=(0, 1))
    grad_mid = grad_two + product("blf,df->bld", grad_pre_b, b_in)
    g_gain_attn = jnp.sum(grad_mid * normed_one, axis=(0, 1))
    g_shift_attn = jnp.sum(grad_mid, axis=(0, 1))
    grad_one = norm_back(grad_mid, normed_one, inv_one, gain_one)
    grad_one_b = grad_one.astype(bf16)
    g_w_out = product("bld,ble->de", context, grad_one_b)
    g_bias_out = jnp.sum(grad_one, axis=(0, 1))
    grad_ctx = (
        product("ble,de->bld", grad_one_b, b_out).astype(bf16).reshape(group, span, HEADS, HEAD_DIM)
    )
    weights_again = jnp.exp(make_scores() - log_total)
    weights_b = weights_again.astype(bf16)
    grad_att = product("bqhe,bkhe->bhqk", grad_ctx, values)
    grad_values = product("bhqk,bqhe->bkhe", weights_b, grad_ctx).reshape(group, span, width)
    delta = jnp.sum(weights_again * grad_att, axis=-1, keepdims=True)
    grad_scores = (weights_again * (grad_att - delta) * scale).astype(bf16)
    grad_query = product("bhqk,bkhe->bqhe", grad_scores, keys).reshape(group, span, width)
    grad_keys = product("bhqk,bqhe->bkhe", grad_scores, query).reshape(group, span, width)
    grad_qkv_b = jnp.concatenate([grad_query, grad_keys, grad_values], axis=-1).astype(bf16)
    g_w_qkv = product("bld,ble->de", inputs, grad_qkv_b)
    g_bias_q = jnp.sum(grad_query, axis=(0, 1))
    g_bias_v = jnp.sum(grad_values, axis=(0, 1))
    grad_input = grad_one + product("ble,de->bld", grad_qkv_b, b_qkv)
    r_back = reduce_weight((g_w_back * factor).astype(bf16), ORDERS[0])
    r_in = reduce_weight((g_w_in * factor).astype(bf16), ORDERS[1])
    r_out = reduce_weight((g_w_out * factor).astype(bf16), ORDERS[2])
    r_qkv = reduce_weight((g_w_qkv * factor).astype(bf16), ORDERS[3])
    r_bq, r_bv, r_bo, r_ga, r_sa, r_bi, r_bb, r_gf, r_sf = reduce_vectors(
        [
            g * factor
            for g in (
                g_bias_q,
                g_bias_v,
                g_bias_out,
                g_gain_attn,
                g_shift_attn,
                g_bias_in,
                g_bias_back,
                g_gain_ffn,
                g_shift_ffn,
            )
        ]
    )
    return (
        block_out.reshape(group * span, width),
        grad_input.reshape(group * span, width),
        r_qkv,
        r_bq,
        r_bv,
        r_out,
        r_bo,
        r_ga,
        r_sa,
        r_in,
        r_bi,
        r_back,
        r_bb,
        r_gf,
        r_sf,
    )


def solution(mesh):
    replicas, shards = mesh.shape["replica"], mesh.shape["shard"]
    mesh = jax.sharding.Mesh(
        mesh.devices.reshape(replicas // 4, 2, 2, shards), ("z", "x", "core", "shard")
    )
    placed = (
        P(("z", "x", "core", "shard"), None),
        P(("z", "x", "core", "shard")),
        P(("z", "x", "core", "shard"), None),
        P("shard", None),
        P("shard"),
        P("shard"),
        P("shard", None),
        P("shard"),
        P("shard"),
        P("shard"),
        P("shard", None),
        P("shard"),
        P("shard", None),
        P("shard"),
        P("shard"),
        P("shard"),
    )
    return jax.shard_map(
        on_device,
        mesh=mesh,
        in_specs=placed,
        out_specs=(
            P(("z", "x", "core", "shard"), None),
            P(("z", "x", "core", "shard"), None),
            P("shard", None),
            P("shard"),
            P("shard"),
            P("shard", None),
            P("shard"),
            P("shard"),
            P("shard"),
            P("shard", None),
            P("shard"),
            P("shard", None),
            P("shard"),
            P("shard"),
            P("shard"),
        ),
        check_vma=False,
    )
```

```python
import jax
import jax.numpy as jnp
from jax import lax
from jax.sharding import PartitionSpec as P

HEADS = 12
HEAD_DIM = 64


def product(form, left, right):
    return jnp.einsum(form, left, right, preferred_element_type=jnp.float32)


def normalize(hidden):
    average = jnp.mean(hidden, axis=-1, keepdims=True)
    centred = hidden - average
    inv_std = lax.rsqrt(jnp.mean(centred * centred, axis=-1, keepdims=True) + 1e-12)
    return (centred * inv_std, inv_std)


def norm_back(grad_in, normed, inv_std, gain):
    grad_norm = grad_in * gain
    return inv_std * (
        grad_norm
        - jnp.mean(grad_norm, axis=-1, keepdims=True)
        - normed * jnp.mean(grad_norm * normed, axis=-1, keepdims=True)
    )


def gelu_slope(pre):
    return (
        0.5 * (1.0 + lax.erf(pre * 0.7071067811865476))
        + pre * jnp.exp(-0.5 * pre * pre) * 0.3989422804014327
    )


def swap(value, axis, size, bit=1):
    return lax.ppermute(value, axis, [(i, i ^ bit) for i in range(size)])


def pick(value, index, dim):
    return lax.dynamic_index_in_dim(value, index, dim, keepdims=True)


def paired(mine, other, bit, dim):
    return jnp.where(
        bit == 0,
        jnp.concatenate([mine, other], axis=dim),
        jnp.concatenate([other, mine], axis=dim),
    )


def gather_weight(block):
    shards = lax.axis_size("shard")
    if shards != 2:
        return lax.all_gather(block, "shard", axis=0, tiled=True)
    rows = block.shape[0]
    here, x, core = lax.axis_index("shard"), lax.axis_index("x"), lax.axis_index("core")
    parts = block.reshape(2, 2, rows // 4, block.shape[1])
    mine = pick(pick(parts, x, 0), core, 1)
    far = swap(mine, "shard", 2)
    far = paired(far, swap(far, "x", 2), x, 0)
    far = paired(far, swap(far, "core", 2), core, 1)
    return paired(block, far.reshape(block.shape), here, 0)


def gather_vectors(vectors, long):
    shards, width = lax.axis_size("shard"), vectors[0].shape[0]
    rows = [v.astype(jnp.float32)[None] for v in vectors]
    packed = jnp.concatenate(rows + [long.astype(jnp.float32).reshape(-1, width)])
    if shards == 2:
        both = paired(packed[None], swap(packed, "shard", 2)[None], lax.axis_index("shard"), 0)
    else:
        both = lax.all_gather(packed, "shard", axis=0)
    count = len(vectors)
    short = both[:, :count].transpose(1, 0, 2).reshape(count, shards * width)
    return [short[i] for i in range(count)] + [both[:, count:].reshape(-1)]


def z_bits():
    return (lax.axis_size("z") - 1).bit_length()


def stage(name):
    if name[0] == "z":
        bit = int(name[1:])
        return "z", lax.axis_size("z"), 1 << bit, (lax.axis_index("z") >> bit) & 1, 3 + bit
    return name, 2, 1, lax.axis_index(name), {"shard": 0, "core": 1, "x": 2}[name]


def split_grad(grad):
    shards, bits = lax.axis_size("shard"), z_bits()
    rows = grad.shape[0] // (shards * 4 * lax.axis_size("z"))
    return grad.reshape((shards, 2, 2) + (2,) * bits + (rows, grad.shape[1]))


def halve(held, names):
    bf16, f32 = jnp.bfloat16, jnp.float32
    for name in names:
        if name == "shard" and lax.axis_size("shard") != 2:
            held = lax.psum_scatter(held.astype(f32), "shard", scatter_dimension=0, tiled=True)
            continue
        axis, size, hop, bit, dim = stage(name)
        arrived = swap(pick(held, 1 - bit, dim).astype(bf16), axis, size, hop)
        held = pick(held, bit, dim).astype(f32) + arrived.astype(f32)
    return held


def double(held, names):
    held = held.astype(jnp.bfloat16)
    for name in names:
        axis, size, hop, bit, dim = stage(name)
        held = paired(held, swap(held, axis, size, hop), bit, dim)
    return held.reshape(-1, held.shape[-1]).astype(jnp.float32)


def tie(*values):
    return lax.optimization_barrier(values)


def reduce_vectors(vectors, long, factor):
    shards, width = lax.axis_size("shard"), vectors[0].shape[0]
    part, count = width // shards, len(vectors)
    tall = long.reshape(shards, -1, part).transpose(1, 0, 2).reshape(-1, width)
    packed = jnp.concatenate([v[None] for v in vectors] + [tall]) * factor
    for name in ["core", "x"] + [f"z{b}" for b in range(z_bits())]:
        axis, size, hop, _, _ = stage(name)
        packed = packed + swap(packed, axis, size, hop)
    here = lax.axis_index("shard")
    if shards == 2:
        own = lax.dynamic_slice_in_dim(packed, here * part, part, 1)
        total = own + swap(lax.dynamic_slice_in_dim(packed, (1 - here) * part, part, 1), "shard", 2)
    else:
        total = lax.psum_scatter(packed, "shard", scatter_dimension=1, tiled=True)
    return [total[i] for i in range(count)] + [total[count:].reshape(-1)]


def on_device(
    tokens,
    lengths,
    cotangent,
    w_qkv,
    bias_q,
    bias_v,
    w_out,
    bias_out,
    gain_attn,
    shift_attn,
    w_in,
    bias_in,
    w_back,
    bias_back,
    gain_ffn,
    shift_ffn,
):
    bf16 = jnp.bfloat16
    f32 = jnp.float32
    f_bq, f_bv, f_bo, f_ga, f_sa, f_bb, f_gf, f_sf, f_bi = gather_vectors(
        (bias_q, bias_v, bias_out, gain_attn, shift_attn, bias_back, gain_ffn, shift_ffn), bias_in
    )
    f_qkv = gather_weight(w_qkv)
    f_out = gather_weight(w_out)
    f_in = gather_weight(w_in)
    f_back = gather_weight(w_back)
    group = lengths.shape[0]
    span = tokens.shape[0] // group
    width = tokens.shape[1]
    scale = HEAD_DIM ** (-0.5)
    factor = float(tokens.shape[0] * lax.axis_size(("z", "x", "core", "shard"))) ** (-0.5)
    live = jnp.arange(span, dtype=jnp.int32)[None, :] < lengths[:, None]
    inputs = tokens.reshape(group, span, width)
    qkv = product("bld,de->ble", inputs, f_qkv)
    query = (qkv[..., :width] + f_bq.astype(f32)).astype(bf16).reshape(group, span, HEADS, HEAD_DIM)
    keys = qkv[..., width : 2 * width].astype(bf16).reshape(group, span, HEADS, HEAD_DIM)
    values = (
        (qkv[..., 2 * width :] + f_bv.astype(f32))
        .astype(bf16)
        .reshape(group, span, HEADS, HEAD_DIM)
    )

    def make_scores():
        raw = product("bqhe,bkhe->bhqk", query, keys) * scale
        return jnp.where(live[:, None, None, :], raw, -1000000000.0)

    scores = make_scores()
    top = jnp.max(scores, axis=-1, keepdims=True)
    expo = jnp.exp(scores - top)
    total = jnp.sum(expo, axis=-1, keepdims=True)
    log_total = top + jnp.log(total)
    attend = (expo / total).astype(bf16)
    context = product("bhqk,bkhe->bqhe", attend, values).reshape(group, span, width).astype(bf16)
    resid_one = inputs.astype(f32) + product("bld,de->ble", context, f_out) + f_bo.astype(f32)
    normed_one, inv_one = normalize(resid_one)
    gain_one = f_ga.astype(f32)
    mid = normed_one * gain_one + f_sa.astype(f32)
    mid_b = mid.astype(bf16)
    pre = product("bld,df->blf", mid_b, f_in) + f_bi.astype(f32)
    act = (0.5 * pre * (1.0 + lax.erf(pre * 0.7071067811865476))).astype(bf16)
    resid_two = mid + product("blf,fd->bld", act, f_back) + f_bb.astype(f32)
    normed_two, inv_two = normalize(resid_two)
    gain_two = f_gf.astype(f32)
    block_out = (normed_two * gain_two + f_sf.astype(f32)).astype(bf16)
    b_qkv, b_out, b_in, b_back = f_qkv, f_out, f_in, f_back
    grad_out = cotangent.reshape(group, span, width).astype(f32) * live[..., None].astype(f32)
    g_gain_ffn = jnp.sum(grad_out * normed_two, axis=(0, 1))
    g_shift_ffn = jnp.sum(grad_out, axis=(0, 1))
    grad_two = norm_back(grad_out, normed_two, inv_two, gain_two)
    grad_two_b = grad_two.astype(bf16)
    g_w_back = product("blf,bld->fd", act, grad_two_b)
    g_bias_back = jnp.sum(grad_two, axis=(0, 1))
    held_back = halve(split_grad((g_w_back * factor).astype(bf16)), ("core",))
    grad_pre = product("bld,fd->blf", grad_two_b, b_back) * gelu_slope(pre)
    grad_pre_b = grad_pre.astype(bf16)
    g_w_in = product("bld,blf->df", mid_b, grad_pre_b)
    g_bias_in = jnp.sum(grad_pre, axis=(0, 1))
    held_in = halve(split_grad((g_w_in * factor).astype(bf16)), ("core",))
    grad_mid = grad_two + product("blf,df->bld", grad_pre_b, b_in)
    g_gain_attn = jnp.sum(grad_mid * normed_one, axis=(0, 1))
    g_shift_attn = jnp.sum(grad_mid, axis=(0, 1))
    grad_one = norm_back(grad_mid, normed_one, inv_one, gain_one)
    grad_one_b = grad_one.astype(bf16)
    grad_one_b, held_back, held_in = tie(grad_one_b, held_back, held_in)
    held_back = halve(held_back, ("shard",))
    held_in = halve(held_in, ("x",))
    g_w_out = product("bld,ble->de", context, grad_one_b)
    g_bias_out = jnp.sum(grad_one, axis=(0, 1))
    grad_ctx = (
        product("ble,de->bld", grad_one_b, b_out).astype(bf16).reshape(group, span, HEADS, HEAD_DIM)
    )
    weights_again = jnp.exp(make_scores() - log_total)
    weights_b = weights_again.astype(bf16)
    grad_att = product("bqhe,bkhe->bhqk", grad_ctx, values)
    grad_values = product("bhqk,bqhe->bkhe", weights_b, grad_ctx).reshape(group, span, width)
    delta = jnp.sum(weights_again * grad_att, axis=-1, keepdims=True)
    grad_scores = (weights_again * (grad_att - delta) * scale).astype(bf16)
    grad_query = product("bhqk,bkhe->bqhe", grad_scores, keys).reshape(group, span, width)
    grad_keys = product("bhqk,bqhe->bkhe", grad_scores, query).reshape(group, span, width)
    grad_qkv_b = jnp.concatenate([grad_query, grad_keys, grad_values], axis=-1).astype(bf16)
    g_w_qkv = product("bld,ble->de", inputs, grad_qkv_b)
    g_bias_q = jnp.sum(grad_query, axis=(0, 1))
    g_bias_v = jnp.sum(grad_values, axis=(0, 1))
    grad_input = grad_one + product("ble,de->bld", grad_qkv_b, b_qkv)
    held_attn = split_grad(
        jnp.concatenate([(g_w_qkv * factor).astype(bf16), (g_w_out * factor).astype(bf16)], axis=1)
    )
    held_attn, held_back, held_in = tie(held_attn, held_back, held_in)
    held_back, held_in, held_attn = tie(
        halve(held_back, ("x",)), halve(held_in, ("shard",)), halve(held_attn, ("core",))
    )
    bits = [f"z{b}" for b in range(z_bits())]
    up = bits[::-1]
    r_attn = double(halve(held_attn, ["shard", "x"] + bits), up + ["x", "core"])
    r_back = double(halve(held_back, bits), up + ["x", "core"])
    r_in = double(halve(held_in, bits), up + ["x", "core"])
    r_qkv, r_out = r_attn[:, : 3 * width], r_attn[:, 3 * width :]
    r_bq, r_bv, r_bo, r_ga, r_sa, r_bb, r_gf, r_sf, r_bi = reduce_vectors(
        (
            g_bias_q,
            g_bias_v,
            g_bias_out,
            g_gain_attn,
            g_shift_attn,
            g_bias_back,
            g_gain_ffn,
            g_shift_ffn,
        ),
        g_bias_in,
        factor,
    )
    return (
        block_out.reshape(group * span, width),
        grad_input.reshape(group * span, width),
        r_qkv,
        r_bq,
        r_bv,
        r_out,
        r_bo,
        r_ga,
        r_sa,
        r_in,
        r_bi,
        r_back,
        r_bb,
        r_gf,
        r_sf,
    )


def solution(mesh):
    replicas, shards = mesh.shape["replica"], mesh.shape["shard"]
    mesh = jax.sharding.Mesh(
        mesh.devices.reshape(replicas // 4, 2, 2, shards), ("z", "x", "core", "shard")
    )
    placed = (
        P(("z", "x", "core", "shard"), None),
        P(("z", "x", "core", "shard")),
        P(("z", "x", "core", "shard"), None),
        P("shard", None),
        P("shard"),
        P("shard"),
        P("shard", None),
        P("shard"),
        P("shard"),
        P("shard"),
        P("shard", None),
        P("shard"),
        P("shard", None),
        P("shard"),
        P("shard"),
        P("shard"),
    )
    return jax.shard_map(
        on_device,
        mesh=mesh,
        in_specs=placed,
        out_specs=(
            P(("z", "x", "core", "shard"), None),
            P(("z", "x", "core", "shard"), None),
            P("shard", None),
            P("shard"),
            P("shard"),
            P("shard", None),
            P("shard"),
            P("shard"),
            P("shard"),
            P("shard", None),
            P("shard"),
            P("shard", None),
            P("shard"),
            P("shard"),
            P("shard"),
        ),
        check_vma=False,
    )
```

```python
import jax
import jax.numpy as jnp
from jax import lax
from jax.sharding import PartitionSpec as P

HEADS = 12
HEAD_DIM = 64


def product(form, left, right):
    return jnp.einsum(form, left, right, preferred_element_type=jnp.float32)


def normalize(hidden):
    average = jnp.mean(hidden, axis=-1, keepdims=True)
    centred = hidden - average
    inv_std = lax.rsqrt(jnp.mean(centred * centred, axis=-1, keepdims=True) + 1e-12)
    return (centred * inv_std, inv_std)


def norm_back(grad_in, normed, inv_std, gain):
    grad_norm = grad_in * gain
    return inv_std * (
        grad_norm
        - jnp.mean(grad_norm, axis=-1, keepdims=True)
        - normed * jnp.mean(grad_norm * normed, axis=-1, keepdims=True)
    )


def gelu_slope(pre):
    return (
        0.5 * (1.0 + lax.erf(pre * 0.7071067811865476))
        + pre * jnp.exp(-0.5 * pre * pre) * 0.3989422804014327
    )


def swap(value, axis, size, bit=1):
    return lax.ppermute(value, axis, [(i, i ^ bit) for i in range(size)])


def pick(value, index, dim):
    return lax.dynamic_index_in_dim(value, index, dim, keepdims=True)


def paired(mine, other, bit, dim):
    return jnp.where(
        bit == 0,
        jnp.concatenate([mine, other], axis=dim),
        jnp.concatenate([other, mine], axis=dim),
    )


def first_hop(block):
    if lax.axis_size("shard") != 2:
        return lax.all_gather(block, "shard", axis=0, tiled=True)
    parts = block.reshape(2, 2, block.shape[0] // 4, block.shape[1])
    mine = pick(pick(parts, lax.axis_index("x"), 0), lax.axis_index("core"), 1)
    return swap(mine, "shard", 2)


def later_hops(block, far):
    if lax.axis_size("shard") != 2:
        return far
    far = paired(far, swap(far, "x", 2), lax.axis_index("x"), 0)
    far = paired(far, swap(far, "core", 2), lax.axis_index("core"), 1)
    return paired(block, far.reshape(block.shape), lax.axis_index("shard"), 0)


def gather_weight(block):
    return later_hops(block, first_hop(block))


def tie_first(w_qkv, w_out, w_in, w_back):
    far_qkv, far_out, w_in, w_back = tie(first_hop(w_qkv), first_hop(w_out), w_in, w_back)
    return later_hops(w_qkv, far_qkv), later_hops(w_out, far_out), w_in, w_back


def gather_vectors(vectors, long):
    shards, width = lax.axis_size("shard"), vectors[0].shape[0]
    rows = [v.astype(jnp.float32)[None] for v in vectors]
    packed = jnp.concatenate(rows + [long.astype(jnp.float32).reshape(-1, width)])
    if shards == 2:
        both = paired(packed[None], swap(packed, "shard", 2)[None], lax.axis_index("shard"), 0)
    else:
        both = lax.all_gather(packed, "shard", axis=0)
    count = len(vectors)
    short = both[:, :count].transpose(1, 0, 2).reshape(count, shards * width)
    return [short[i] for i in range(count)] + [both[:, count:].reshape(-1)]


def z_bits():
    return (lax.axis_size("z") - 1).bit_length()


def stage(name):
    if name[0] == "z":
        bit = int(name[1:])
        return "z", lax.axis_size("z"), 1 << bit, (lax.axis_index("z") >> bit) & 1, 3 + bit
    return name, 2, 1, lax.axis_index(name), {"shard": 0, "core": 1, "x": 2}[name]


def split_grad(grad):
    shards, bits = lax.axis_size("shard"), z_bits()
    rows = grad.shape[0] // (shards * 4 * lax.axis_size("z"))
    return grad.reshape((shards, 2, 2) + (2,) * bits + (rows, grad.shape[1]))


def halve(held, names):
    bf16, f32 = jnp.bfloat16, jnp.float32
    for name in names:
        if name == "shard" and lax.axis_size("shard") != 2:
            held = lax.psum_scatter(held.astype(f32), "shard", scatter_dimension=0, tiled=True)
            continue
        axis, size, hop, bit, dim = stage(name)
        arrived = swap(pick(held, 1 - bit, dim).astype(bf16), axis, size, hop)
        held = pick(held, bit, dim).astype(f32) + arrived.astype(f32)
    return held


def double(held, names):
    held = held.astype(jnp.bfloat16)
    for name in names:
        axis, size, hop, bit, dim = stage(name)
        held = paired(held, swap(held, axis, size, hop), bit, dim)
    return held.reshape(-1, held.shape[-1]).astype(jnp.float32)


def tie(*values):
    return lax.optimization_barrier(values)


def reduce_vectors(vectors, long, factor):
    shards, width = lax.axis_size("shard"), vectors[0].shape[0]
    part, count = width // shards, len(vectors)
    tall = long.reshape(shards, -1, part).transpose(1, 0, 2).reshape(-1, width)
    packed = jnp.concatenate([v[None] for v in vectors] + [tall]) * factor
    for name in ["core", "x"] + [f"z{b}" for b in range(z_bits())]:
        axis, size, hop, _, _ = stage(name)
        packed = packed + swap(packed, axis, size, hop)
    here = lax.axis_index("shard")
    if shards == 2:
        own = lax.dynamic_slice_in_dim(packed, here * part, part, 1)
        total = own + swap(lax.dynamic_slice_in_dim(packed, (1 - here) * part, part, 1), "shard", 2)
    else:
        total = lax.psum_scatter(packed, "shard", scatter_dimension=1, tiled=True)
    return [total[i] for i in range(count)] + [total[count:].reshape(-1)]


def on_device(
    tokens,
    lengths,
    cotangent,
    w_qkv,
    bias_q,
    bias_v,
    w_out,
    bias_out,
    gain_attn,
    shift_attn,
    w_in,
    bias_in,
    w_back,
    bias_back,
    gain_ffn,
    shift_ffn,
):
    bf16 = jnp.bfloat16
    f32 = jnp.float32
    f_bq, f_bv, f_bo, f_ga, f_sa, f_bb, f_gf, f_sf, f_bi = gather_vectors(
        (bias_q, bias_v, bias_out, gain_attn, shift_attn, bias_back, gain_ffn, shift_ffn), bias_in
    )
    f_qkv, f_out, w_in, w_back = tie_first(w_qkv, w_out, w_in, w_back)
    f_in = gather_weight(w_in)
    f_back = gather_weight(w_back)
    group = lengths.shape[0]
    span = tokens.shape[0] // group
    width = tokens.shape[1]
    scale = HEAD_DIM ** (-0.5)
    factor = float(tokens.shape[0] * lax.axis_size(("z", "x", "core", "shard"))) ** (-0.5)
    live = jnp.arange(span, dtype=jnp.int32)[None, :] < lengths[:, None]
    inputs = tokens.reshape(group, span, width)
    qkv = product("bld,de->ble", inputs, f_qkv)
    query = (qkv[..., :width] + f_bq.astype(f32)).astype(bf16).reshape(group, span, HEADS, HEAD_DIM)
    keys = qkv[..., width : 2 * width].astype(bf16).reshape(group, span, HEADS, HEAD_DIM)
    values = (
        (qkv[..., 2 * width :] + f_bv.astype(f32))
        .astype(bf16)
        .reshape(group, span, HEADS, HEAD_DIM)
    )

    def make_scores():
        raw = product("bqhe,bkhe->bhqk", query, keys) * scale
        return jnp.where(live[:, None, None, :], raw, -1000000000.0)

    scores = make_scores()
    top = jnp.max(scores, axis=-1, keepdims=True)
    expo = jnp.exp(scores - top)
    total = jnp.sum(expo, axis=-1, keepdims=True)
    log_total = top + jnp.log(total)
    attend = (expo / total).astype(bf16)
    context = product("bhqk,bkhe->bqhe", attend, values).reshape(group, span, width).astype(bf16)
    resid_one = inputs.astype(f32) + product("bld,de->ble", context, f_out) + f_bo.astype(f32)
    normed_one, inv_one = normalize(resid_one)
    gain_one = f_ga.astype(f32)
    mid = normed_one * gain_one + f_sa.astype(f32)
    mid_b = mid.astype(bf16)
    pre = product("bld,df->blf", mid_b, f_in) + f_bi.astype(f32)
    act = (0.5 * pre * (1.0 + lax.erf(pre * 0.7071067811865476))).astype(bf16)
    resid_two = mid + product("blf,fd->bld", act, f_back) + f_bb.astype(f32)
    normed_two, inv_two = normalize(resid_two)
    gain_two = f_gf.astype(f32)
    block_out = (normed_two * gain_two + f_sf.astype(f32)).astype(bf16)
    b_qkv, b_out, b_in, b_back = f_qkv, f_out, f_in, f_back
    grad_out = cotangent.reshape(group, span, width).astype(f32) * live[..., None].astype(f32)
    g_gain_ffn = jnp.sum(grad_out * normed_two, axis=(0, 1))
    g_shift_ffn = jnp.sum(grad_out, axis=(0, 1))
    grad_two = norm_back(grad_out, normed_two, inv_two, gain_two)
    grad_two_b = grad_two.astype(bf16)
    g_w_back = product("blf,bld->fd", act, grad_two_b)
    g_bias_back = jnp.sum(grad_two, axis=(0, 1))
    held_back = halve(split_grad((g_w_back * factor).astype(bf16)), ("core",))
    grad_pre = product("bld,fd->blf", grad_two_b, b_back) * gelu_slope(pre)
    grad_pre_b = grad_pre.astype(bf16)
    g_w_in = product("bld,blf->df", mid_b, grad_pre_b)
    g_bias_in = jnp.sum(grad_pre, axis=(0, 1))
    held_in = halve(split_grad((g_w_in * factor).astype(bf16)), ("core",))
    grad_mid = grad_two + product("blf,df->bld", grad_pre_b, b_in)
    g_gain_attn = jnp.sum(grad_mid * normed_one, axis=(0, 1))
    g_shift_attn = jnp.sum(grad_mid, axis=(0, 1))
    grad_one = norm_back(grad_mid, normed_one, inv_one, gain_one)
    grad_one_b = grad_one.astype(bf16)
    grad_one_b, held_back, held_in = tie(grad_one_b, held_back, held_in)
    held_back = halve(held_back, ("shard",))
    held_in = halve(held_in, ("x",))
    g_w_out = product("bld,ble->de", context, grad_one_b)
    g_bias_out = jnp.sum(grad_one, axis=(0, 1))
    grad_ctx = (
        product("ble,de->bld", grad_one_b, b_out).astype(bf16).reshape(group, span, HEADS, HEAD_DIM)
    )
    weights_again = jnp.exp(make_scores() - log_total)
    weights_b = weights_again.astype(bf16)
    grad_att = product("bqhe,bkhe->bhqk", grad_ctx, values)
    grad_values = product("bhqk,bqhe->bkhe", weights_b, grad_ctx).reshape(group, span, width)
    delta = jnp.sum(weights_again * grad_att, axis=-1, keepdims=True)
    grad_scores = (weights_again * (grad_att - delta) * scale).astype(bf16)
    grad_scores, held_back, held_in = tie(grad_scores, held_back, held_in)
    held_back = halve(held_back, ("x",))
    held_in = halve(held_in, ("shard",))
    grad_query = product("bhqk,bkhe->bqhe", grad_scores, keys).reshape(group, span, width)
    grad_keys = product("bhqk,bqhe->bkhe", grad_scores, query).reshape(group, span, width)
    grad_qkv_b = jnp.concatenate([grad_query, grad_keys, grad_values], axis=-1).astype(bf16)
    g_w_qkv = product("bld,ble->de", inputs, grad_qkv_b)
    g_bias_q = jnp.sum(grad_query, axis=(0, 1))
    g_bias_v = jnp.sum(grad_values, axis=(0, 1))
    grad_input = grad_one + product("ble,de->bld", grad_qkv_b, b_qkv)
    held_attn = split_grad(
        jnp.concatenate([(g_w_qkv * factor).astype(bf16), (g_w_out * factor).astype(bf16)], axis=1)
    )
    held_attn, held_back, held_in = tie(held_attn, held_back, held_in)
    bits = [f"z{b}" for b in range(z_bits())]
    held_back, held_in, held_attn, g_bias_q = tie(
        halve(held_back, bits[:1]), halve(held_in, bits[:1]), halve(held_attn, ("core",)), g_bias_q
    )
    up = bits[::-1]
    r_attn = double(halve(held_attn, ["shard", "x"] + bits), up + ["x", "core"])
    r_back = double(halve(held_back, bits[1:]), up + ["x", "core"])
    r_in = double(halve(held_in, bits[1:]), up + ["x", "core"])
    r_qkv, r_out = r_attn[:, : 3 * width], r_attn[:, 3 * width :]
    r_bq, r_bv, r_bo, r_ga, r_sa, r_bb, r_gf, r_sf, r_bi = reduce_vectors(
        (
            g_bias_q,
            g_bias_v,
            g_bias_out,
            g_gain_attn,
            g_shift_attn,
            g_bias_back,
            g_gain_ffn,
            g_shift_ffn,
        ),
        g_bias_in,
        factor,
    )
    return (
        block_out.reshape(group * span, width),
        grad_input.reshape(group * span, width),
        r_qkv,
        r_bq,
        r_bv,
        r_out,
        r_bo,
        r_ga,
        r_sa,
        r_in,
        r_bi,
        r_back,
        r_bb,
        r_gf,
        r_sf,
    )


def solution(mesh):
    replicas, shards = mesh.shape["replica"], mesh.shape["shard"]
    mesh = jax.sharding.Mesh(
        mesh.devices.reshape(replicas // 4, 2, 2, shards), ("z", "x", "core", "shard")
    )
    placed = (
        P(("z", "x", "core", "shard"), None),
        P(("z", "x", "core", "shard")),
        P(("z", "x", "core", "shard"), None),
        P("shard", None),
        P("shard"),
        P("shard"),
        P("shard", None),
        P("shard"),
        P("shard"),
        P("shard"),
        P("shard", None),
        P("shard"),
        P("shard", None),
        P("shard"),
        P("shard"),
        P("shard"),
    )
    return jax.shard_map(
        on_device,
        mesh=mesh,
        in_specs=placed,
        out_specs=(
            P(("z", "x", "core", "shard"), None),
            P(("z", "x", "core", "shard"), None),
            P("shard", None),
            P("shard"),
            P("shard"),
            P("shard", None),
            P("shard"),
            P("shard"),
            P("shard"),
            P("shard", None),
            P("shard"),
            P("shard", None),
            P("shard"),
            P("shard"),
            P("shard"),
        ),
        check_vma=False,
    )
```
